32 devices in a mesh: dp: 8 (over z, y), fsdp: 4 (over x, core).
Axes of the slice: x: 2, y: 2, z: 4, core: 2. Of those that a mesh axis runs over, the one named last changes fastest.
Arguments:
- hidden_in: float32 [8192, 768], P(('dp', 'fsdp')), may hold values from -6 to 6
- cotangent: float32 [8192, 768], P(('dp', 'fsdp')), may hold values from -6 to 6
- seq_ids: int32 [8192], P(('dp', 'fsdp')), may hold values from -1 to 8191, as said below
- norm_gain: bfloat16 [768], P(('dp', 'fsdp')), may hold values from 0.5 to 1.5
- in_weight: bfloat16 [768, 3352], P(('dp', 'fsdp')), may hold values from -0.21875 to 0.21875
- conv_weight: bfloat16 [4, 1792], P(None, ('dp', 'fsdp')), may hold values from -3 to 3
- conv_bias: bfloat16 [1792], P(('dp', 'fsdp')), may hold values from -3 to 3
- out_gain: bfloat16 [1536], P(('dp', 'fsdp')), may hold values from 0.5 to 1.5
- out_weight: bfloat16 [1536, 768], P(('dp', 'fsdp')), may hold values from -0.15625 to 0.15625
- decay_log: float32 [24], replicated, may hold values from 0 to 2.77
- skip_gain: float32 [24], replicated, may hold values from 0.5 to 1.5
- step_bias: float32 [24], replicated, may hold values from -4.6 to -0.5
Outputs:
- block_out: float32 [8192, 768], P(('dp', 'fsdp'))
- grad_hidden: float32 [8192, 768], P(('dp', 'fsdp'))
- grad_norm_gain: float32 [768], P(('dp', 'fsdp'))
- grad_in_weight: float32 [768, 3352], P(('dp', 'fsdp'))
- grad_conv_weight: float32 [4, 1792], P(None, ('dp', 'fsdp'))
- grad_conv_bias: float32 [1792], P(('dp', 'fsdp'))
- grad_out_gain: float32 [1536], P(('dp', 'fsdp'))
- grad_out_weight: float32 [1536, 768], P(('dp', 'fsdp'))
- grad_decay_log: float32 [24], replicated
- grad_skip_gain: float32 [24], replicated
- grad_step_bias: float32 [24], replicated
The draws below stay inside these ranges and needn't reach their ends.
Inputs may be any that keep to these rules, and one draw needn't show every extreme that they name: `seq_ids`: in each aligned block of 256 slots the live slots come first and the rest hold -1; a sequence fills consecutive slots inside one block and its numbers rise along the slots; a sequence has at most 256 tokens, and some sequence has exactly 256; the first block has no empty slot.
All inputs are finite; a program needn't handle non-finite values.
Results may differ from the reference program's by a relative error of at most 0.015.
Values may be sent and summed in bfloat16 or wider, within the bound.
A program may use at most 128 MiB of HBM per device.

```python
from functools import partial
import jax
import jax.numpy as jnp
from jax import lax

D = 768
NS = 128
HD = 64
NH = 24
KC = 4
SPAN = 128
SEQ_MAX = 256
TOK_DEV = 256
DI = 1536
CONV = 1792
DIN = 3352
TOKENS = 8192


def draw_seq_ids(key, part):
    groups = TOKENS // TOK_DEV
    count_key, start_key = jax.random.split(jax.random.fold_in(key, 7))
    counts = jax.random.randint(count_key, (groups,), TOK_DEV // 4, TOK_DEV + 1)
    counts = jnp.where(jnp.arange(groups) == 0, TOK_DEV, counts)
    slots = jnp.arange(TOK_DEV)[None, :]
    group_row = jnp.arange(groups)[:, None]
    starts = jax.random.randint(start_key, (groups, TOK_DEV), 0, 96) == 0
    starts = starts | (slots % SEQ_MAX == 0)
    starts = starts & ~((group_row == 0) & (slots % SEQ_MAX != 0))
    number = jnp.cumsum(starts.astype(jnp.int32), axis=1) - 1 + group_row * TOK_DEV
    return jnp.where(slots < counts[:, None], number, -1).reshape(-1).astype(jnp.int32)


def levels(key, dims, cuts, smallest, high):
    def one(axis_at, parts):
        draws = jax.random.uniform(jax.random.fold_in(jax.random.fold_in(key, 6), axis_at), (parts,), jnp.float32, smallest / len(cuts), high / len(cuts))
        return jnp.repeat(jnp.exp(draws), dims[axis_at] // parts).reshape((-1,) + (1,) * (len(dims) - axis_at - 1))

    loudness = one(*cuts[0])
    for cut in cuts[1:]:
        loudness = loudness * one(*cut)
    return loudness


def gaussian(key, shape, deviation, bound, shards=(), held_as=jnp.bfloat16):
    values = jax.random.normal(key, shape, jnp.float32) * deviation
    if len(shards) > 0:
        values = levels(key, shape, shards, -0.22, 0.18) * values
    return jnp.clip(values, min=-bound, max=bound).astype(held_as)


def setup_inputs(seed: int = 0) -> dict:
    streams_of = jax.random.split(jax.random.key(seed), 13)
    hidden_in = gaussian(streams_of[0], (TOKENS, D), 1.0, 6.0, ((0, 32),), jnp.float32)
    cotangent = gaussian(streams_of[1], (TOKENS, D), 1.0, 6.0, ((0, 32),), jnp.float32)
    seq_ids = draw_seq_ids(jax.random.fold_in(streams_of[12], 71), 0)
    norm_gain = jnp.clip(1.0 + 0.1 * jax.random.normal(streams_of[3], (D,), jnp.float32), 0.5, 1.5).astype(jnp.bfloat16)
    in_weight = gaussian(streams_of[4], (D, DIN), D ** -0.5, 0.21875, ((0, 32),))
    conv_weight = gaussian(streams_of[5], (KC, CONV), KC ** -0.5, 3.0, ((1, 32),))
    conv_bias = gaussian(streams_of[6], (CONV,), 0.5, 3.0, ((0, 32),))
    out_gain = jnp.clip(1.0 + 0.1 * jax.random.normal(streams_of[7], (DI,), jnp.float32), 0.5, 1.5).astype(jnp.bfloat16)
    out_weight = gaussian(streams_of[8], (DI, D), DI ** -0.5, 0.15625, ((0, 32),))
    decay_log = jnp.clip(jax.random.uniform(streams_of[9], (NH,), jnp.float32, 0.0, 2.77), 0.0, 2.77)
    skip_gain = jnp.clip(jax.random.uniform(streams_of[10], (NH,), jnp.float32, 0.5, 1.5), 0.5, 1.5)
    step_bias = jnp.clip(jax.random.uniform(streams_of[11], (NH,), jnp.float32, -4.6, -0.5), -4.6, -0.5)
    return dict(hidden_in=hidden_in, cotangent=cotangent, seq_ids=seq_ids, norm_gain=norm_gain, in_weight=in_weight, conv_weight=conv_weight, conv_bias=conv_bias, out_gain=out_gain, out_weight=out_weight, decay_log=decay_log, skip_gain=skip_gain, step_bias=step_bias)


EPS = 1e-05

def norm_input(hidden, gain):
    scale = lax.rsqrt(lax.optimization_barrier(jnp.mean(hidden * hidden, axis=-1, keepdims=True)) + EPS)
    return hidden * scale * gain[None, :]

def mixer(projected, conv_kernel, conv_shift, out_scale, decay_log, skip_gain, step_bias, seq_index):
    length = projected.shape[0]
    gate_part = projected[:, :DI]
    conv_in = projected[:, DI:DI + CONV]
    step_raw = projected[:, DI + CONV:]
    live_rows = (seq_index >= 0).astype(jnp.float32)
    summed = conv_shift[None, :] + conv_in * conv_kernel[KC - 1][None, :]
    for offset in range(1, KC):
        earlier = jnp.concatenate([jnp.zeros((offset, CONV), jnp.float32), conv_in[:length - offset]], axis=0)
        matched = (seq_index[offset:] == seq_index[:length - offset]).astype(jnp.float32)
        same_seq = jnp.concatenate([jnp.zeros((offset,), jnp.float32), matched], axis=0)
        summed = summed + earlier * same_seq[:, None] * conv_kernel[KC - 1 - offset][None, :]
    activated = jax.nn.silu(summed)
    values = activated[:, :DI]
    in_state = activated[:, DI:DI + NS]
    out_state = activated[:, DI + NS:]
    step_size = jax.nn.softplus(step_raw + step_bias[None, :])
    log_decay = step_size * (-jnp.exp(decay_log))[None, :]
    blocks = length // SPAN
    scaled = (values.reshape(length, NH, HD) * step_size[:, :, None]).reshape(blocks, SPAN, NH, HD)
    keys_in = in_state.reshape(blocks, SPAN, NS)
    query_out = out_state.reshape(blocks, SPAN, NS)
    seq_blocks = seq_index.reshape(blocks, SPAN)
    running = jnp.cumsum(log_decay.reshape(blocks, SPAN, NH), axis=1).transpose(0, 2, 1)
    row_pos = lax.broadcasted_iota(jnp.int32, (SPAN, SPAN), 0)
    col_pos = lax.broadcasted_iota(jnp.int32, (SPAN, SPAN), 1)
    causal = (row_pos >= col_pos).astype(jnp.float32)
    pair_mask = (seq_blocks[:, :, None] == seq_blocks[:, None, :]).astype(jnp.float32) * causal[None]
    intersection = jnp.einsum('cqn,csn->cqs', query_out, keys_in, precision=lax.Precision.HIGHEST)
    gaps = running[:, :, :, None] - running[:, :, None, :]
    decays = jnp.exp(gaps * pair_mask[:, None]) * pair_mask[:, None]
    mixing = decays * intersection[:, None]
    inner_out = jnp.einsum('chqs,cshp->cqhp', mixing, scaled, precision=lax.Precision.HIGHEST)
    last_seq = seq_blocks[:, -1]
    end_total = running[:, :, -1]
    tail_mask = (seq_blocks == last_seq[:, None]).astype(jnp.float32)
    to_end = jnp.exp((end_total[:, :, None] - running) * tail_mask[:, None]) * tail_mask[:, None]
    block_state = jnp.einsum('csn,chs,cshp->chnp', keys_in, to_end, scaled, precision=lax.Precision.HIGHEST)
    prior_seq = jnp.concatenate([jnp.full((1,), -2, jnp.int32), last_seq[:-1].astype(jnp.int32)])
    carried = (last_seq == prior_seq).astype(jnp.float32)

    def advance(state, inputs):
        fresh, factor, flag = inputs
        return (state * factor[:, None, None] * flag + fresh, state)
    _, incoming = lax.scan(advance, jnp.zeros((NH, NS, HD), jnp.float32), (block_state, jnp.exp(end_total), carried))
    entering = (seq_blocks == prior_seq[:, None]).astype(jnp.float32)
    from_state = jnp.einsum('cqn,chnp->cqhp', query_out, incoming, precision=lax.Precision.HIGHEST)
    growth = jnp.exp(running).transpose(0, 2, 1) * entering[:, :, None]
    result = (inner_out + from_state * growth[:, :, :, None]).reshape(length, NH, HD)
    result = result + skip_gain[None, :, None] * values.reshape(length, NH, HD)
    gated = result.reshape(length, DI) * jax.nn.silu(gate_part)
    scale = lax.rsqrt(lax.optimization_barrier(jnp.mean(gated * gated, axis=-1, keepdims=True)) + EPS)
    return gated * scale * out_scale[None, :] * live_rows[:, None]

def rounded(value):
    return lax.optimization_barrier(value.astype(jnp.bfloat16)).astype(jnp.float32)

def reference(hidden_in, cotangent, seq_ids, norm_gain, in_weight, conv_weight, conv_bias, out_gain, out_weight, decay_log, skip_gain, step_bias):
    groups = TOKENS // TOK_DEV
    gain_in = norm_gain.astype(jnp.float32)
    kernel = conv_weight.astype(jnp.float32)
    shift = conv_bias.astype(jnp.float32)
    gain_out = out_gain.astype(jnp.float32)
    contract_rows = (((0,), (0,)), ((), ()))
    contract_cols = (((1,), (1,)), ((), ()))

    def one_block(totals, inputs):
        hidden, upstream, seq_index = inputs
        normed, norm_pull = jax.vjp(norm_input, hidden, gain_in)
        normed_b = normed.astype(jnp.bfloat16)
        projected = jnp.dot(normed_b, in_weight, preferred_element_type=jnp.float32)
        mixed_out, mix_pull = jax.vjp(partial(mixer, seq_index=seq_index), projected, kernel, shift, gain_out, decay_log, skip_gain, step_bias)
        mixed_b = mixed_out.astype(jnp.bfloat16)
        output = hidden + jnp.dot(mixed_b, out_weight, preferred_element_type=jnp.float32)
        upstream_b = upstream.astype(jnp.bfloat16)
        grad_wout = lax.dot_general(mixed_b, upstream_b, contract_rows, preferred_element_type=jnp.float32)
        d_mixed = lax.dot_general(upstream_b, out_weight, contract_cols, preferred_element_type=jnp.float32)
        pulled = mix_pull(d_mixed)
        d_proj_b = pulled[0].astype(jnp.bfloat16)
        grad_win = lax.dot_general(normed_b, d_proj_b, contract_rows, preferred_element_type=jnp.float32)
        d_normed = lax.dot_general(d_proj_b, in_weight, contract_cols, preferred_element_type=jnp.float32)
        d_hidden, grad_gain = norm_pull(d_normed)
        new_totals = (totals[0] + rounded(grad_gain), totals[1] + rounded(grad_win), totals[2] + rounded(pulled[1]), totals[3] + rounded(pulled[2]), totals[4] + rounded(pulled[3]), totals[5] + rounded(grad_wout), totals[6] + pulled[4], totals[7] + pulled[5], totals[8] + pulled[6])
        return (new_totals, (output, upstream + d_hidden))
    start = (jnp.zeros((D,), jnp.float32), jnp.zeros((D, DIN), jnp.float32), jnp.zeros((KC, CONV), jnp.float32), jnp.zeros((CONV,), jnp.float32), jnp.zeros((DI,), jnp.float32), jnp.zeros((DI, D), jnp.float32), jnp.zeros((NH,), jnp.float32), jnp.zeros((NH,), jnp.float32), jnp.zeros((NH,), jnp.float32))
    totals, outputs = lax.scan(one_block, start, (hidden_in.reshape(groups, TOK_DEV, D), cotangent.reshape(groups, TOK_DEV, D), seq_ids.reshape(groups, TOK_DEV)))
    return (outputs[0].reshape(TOKENS, D), outputs[1].reshape(TOKENS, D), totals[0], totals[1], totals[2], totals[3], totals[4], totals[5], totals[6], totals[7], totals[8])
```

```python
import jax
import jax.numpy as jnp
from jax import lax
from jax.experimental import pallas as pl
from jax.experimental.pallas import tpu as pltpu
from jax.sharding import PartitionSpec as P

NS = 128
HD = 64
NH = 24
KC = 4
DI = 1536
CONV = 1792
LANE = 128
EPS = 1e-05
AXES = ("dp", "fsdp")
F32 = jnp.float32
BF16 = jnp.bfloat16
HIGH = lax.Precision.HIGHEST
VM = pl.BlockSpec(memory_space=pltpu.VMEM)


def sds(*shape, dtype=F32):
    return jax.ShapeDtypeStruct(shape, dtype)


def cols(k, width=LANE):
    return pl.ds(pl.multiple_of(k * width, LANE), width)


def sigmoid(x):
    return 1.0 / (1.0 + jnp.exp(-x))


def dot(a, b, dims=((1,), (0,)), precision=None):
    return lax.dot_general(
        a, b, (dims, ((), ())), precision=precision, preferred_element_type=F32
    )


def pair_masks():
    lane = lax.broadcasted_iota(jnp.int32, (1, LANE), 1)
    first = (lane < HD).astype(F32)
    return first, 1.0 - first


def spread(width_from, k):
    head = lax.broadcasted_iota(jnp.int32, (width_from, LANE), 0)
    lane = lax.broadcasted_iota(jnp.int32, (width_from, LANE), 1)
    return (head == 2 * k + lane // HD).astype(F32)


def pair_decay(cum_e, cum_t, k, mask):
    two = cum_e[:, cols(k)]
    low = jnp.float32(-1e30)
    first = two[:, 0:1] - cum_t[pl.ds(2 * k, 1), :]
    second = two[:, HD : HD + 1] - cum_t[pl.ds(2 * k + 1, 1), :]
    return jnp.exp(jnp.where(mask, first, low)), jnp.exp(jnp.where(mask, second, low))


def same_mask(seq_col, seq_row):
    n = seq_col.shape[0]
    row = lax.broadcasted_iota(jnp.int32, (n, n), 0)
    col = lax.broadcasted_iota(jnp.int32, (n, n), 1)
    return (seq_col[...] == seq_row[...]) & (row >= col)


def forward_kernel(
    hidden, w_in, gain, taps, out_gain, skip_e, heads, meta, seq_col, seq_row,
    normed_b, proj, act, d_act, inner, mixed_b, gated, stats, step, step_e, cum_e, cum_t, scores,
):
    h = hidden[...]
    n, d = h.shape
    root = lax.rsqrt(jnp.sum(h * h, axis=-1, keepdims=True) / d + EPS)
    nb = (h * root * gain[...]).astype(BF16)
    normed_b[...] = nb
    wide = 3 * LANE

    @pl.loop(0, proj.shape[1] // wide)
    def _(k):
        proj[:, cols(k, wide)] = dot(nb, w_in[:, cols(k, wide)])

    same = [meta[:, j : j + 1] for j in range(KC - 1)]

    @pl.loop(0, CONV // LANE)
    def _(k):
        x = proj[:, cols(k + DI // LANE)]
        tap = taps[:, cols(k)]
        total = tap[KC : KC + 1] + x * tap[KC - 1 : KC]
        for j in range(1, KC):
            total = total + pltpu.roll(x, j, 0) * same[j - 1] * tap[KC - 1 - j : KC - j]
        sg = sigmoid(total)
        act[:, cols(k)] = total * sg
        d_act[:, cols(k)] = sg * (1.0 + total * (1.0 - sg))

    mask = same_mask(seq_col, seq_row)
    raw = proj[:, DI + CONV : DI + CONV + LANE] + heads[0:1]
    lane = lax.broadcasted_iota(jnp.int32, (1, LANE), 1)
    size = jnp.where(
        lane < NH, jnp.maximum(raw, 0.0) + jnp.log1p(jnp.exp(-jnp.abs(raw))), 0.0
    )
    step[...] = size
    running = dot(mask.astype(F32), size * heads[1:2], precision=HIGH)
    cum_t[...] = running.T
    b = act[:, DI : DI + NS].astype(BF16)
    c = act[:, DI + NS : DI + 2 * NS].astype(BF16)
    scores[...] = dot(c, b, ((1,), (1,)))
    first, second = pair_masks()
    stats[...] = jnp.zeros_like(stats)

    @pl.loop(0, NH // 2)
    def _(k):
        e = spread(LANE, k)
        cum_e[:, cols(k)] = dot(running, e, precision=HIGH)
        size_e = dot(size, e, precision=HIGH)
        step_e[:, cols(k)] = size_e
        decay0, decay1 = pair_decay(cum_e, cum_t, k, mask)
        v = act[:, cols(k)]
        x = v * size_e
        s = scores[...]
        y = dot((s * decay0).astype(BF16), (x * first).astype(BF16)) + dot(
            (s * decay1).astype(BF16), (x * second).astype(BF16)
        )
        inner[:, cols(k)] = y
        g = proj[:, cols(k)]
        z = (y + skip_e[:, cols(k)] * v) * g * sigmoid(g)
        gated[:, cols(k)] = z
        stats[...] += z * z

    scale = lax.rsqrt(jnp.sum(stats[...], axis=-1, keepdims=True) / DI + EPS)
    live = meta[:, KC - 1 : KC]
    stats[...] = jnp.where(lane < HD, scale, root)
    factor = scale * live

    @pl.loop(0, NH // 2)
    def _(k):
        mixed_b[:, cols(k)] = (gated[:, cols(k)] * factor * out_gain[:, cols(k)]).astype(BF16)


def backward_kernel(
    hidden, upstream, w_in, w_out, gain, taps, out_gain, skip_e, heads, meta, seq_col, seq_row,
    proj, act, d_act, inner, gated, stats, step, step_e, cum_e, cum_t, scores,
    grad_hidden, d_proj_b, g_gain, g_taps, g_out, g_heads,
    d_val, d_gated, acc, d_scores,
):
    h = hidden[...]
    n, d = h.shape
    up = upstream[...].astype(BF16)
    mask = same_mask(seq_col, seq_row)
    live = meta[:, KC - 1 : KC]
    scale = stats[:, 0:1]
    root = stats[:, HD : HD + 1]
    first, second = pair_masks()
    acc[...] = jnp.zeros_like(acc)

    @pl.loop(0, NH // 2)
    def _(k):
        dm = dot(up, w_out[cols(k), :], ((1,), (1,))) * live
        z = gated[:, cols(k)]
        g_out[:, cols(k)] = jnp.sum(dm * z * scale, axis=0, keepdims=True)
        u = dm * out_gain[:, cols(k)]
        d_gated[:, cols(k)] = u
        acc[...] += u * z

    pull = jnp.sum(acc[...], axis=-1, keepdims=True) * (scale * scale * scale) / DI
    d_scores[...] = jnp.zeros_like(d_scores)
    g_heads[...] = jnp.zeros_like(g_heads)
    tall = lax.broadcasted_iota(jnp.int32, (8, 1), 0)

    def body(k, carry):
        d_cum, d_step = carry
        e = spread(LANE, k)
        dz = scale * d_gated[:, cols(k)] - gated[:, cols(k)] * pull
        g = proj[:, cols(k)]
        sg = sigmoid(g)
        v = act[:, cols(k)]
        y = inner[:, cols(k)]
        skip = skip_e[:, cols(k)]
        d_proj_b[:, cols(k)] = (
            dz * (y + skip * v) * sg * (1.0 + g * (1.0 - sg))
        ).astype(BF16)
        dy = dz * g * sg
        size_e = step_e[:, cols(k)]
        x = (v * size_e).astype(BF16)
        dyb = dy.astype(BF16)
        dy0 = (dy * first).astype(BF16)
        dy1 = (dy * second).astype(BF16)
        decay0, decay1 = pair_decay(cum_e, cum_t, k, mask)
        s = scores[...]
        dx = dot((s * decay0).astype(BF16), dy0, ((0,), (0,))) + dot(
            (s * decay1).astype(BF16), dy1, ((0,), (0,))
        )
        d_scores[...] += dot(dy0, x, ((1,), (1,))) * decay0 + dot(dy1, x, ((1,), (1,))) * decay1
        d_val[:, cols(k)] = dx * size_e + skip * dy
        flow = dyb.astype(F32) * y - x.astype(F32) * dx
        d_cum = d_cum + dot(flow, e, ((1,), (1,)), precision=HIGH)
        d_step = d_step + dot(dx * v, e, ((1,), (1,)), precision=HIGH)
        skips = jnp.sum(dy * v, axis=0, keepdims=True)
        g_heads[...] += jnp.where(
            tall == 1, dot(jnp.broadcast_to(skips, (8, LANE)), e, ((1,), (1,)), precision=HIGH), 0.0
        )
        return d_cum, d_step

    zero = jnp.zeros((n, LANE), F32)
    d_cum, d_step = lax.fori_loop(0, NH // 2, body, (zero, zero))
    d_rate = dot(mask.astype(F32), d_cum, ((0,), (0,)), precision=HIGH)
    neg = heads[1:2]
    size = step[...]
    raw = proj[:, DI + CONV : DI + CONV + LANE] + heads[0:1]
    lane = lax.broadcasted_iota(jnp.int32, (1, LANE), 1)
    d_raw = jnp.where(lane < NH, (d_step + d_rate * neg) * sigmoid(raw), 0.0)
    d_proj_b[:, DI + CONV : DI + CONV + LANE] = d_raw.astype(BF16)
    g_decay = jnp.sum(d_rate * size * neg, axis=0, keepdims=True)
    g_step = jnp.sum(d_raw, axis=0, keepdims=True)
    g_heads[...] += jnp.where(tall == 0, g_decay, 0.0) + jnp.where(tall == 2, g_step, 0.0)

    b = act[:, DI : DI + NS].astype(BF16)
    c = act[:, DI + NS : DI + 2 * NS].astype(BF16)
    ds = d_scores[...].astype(BF16)
    d_val[:, DI : DI + NS] = dot(ds, c, ((0,), (0,)))
    d_val[:, DI + NS : DI + 2 * NS] = dot(ds, b)
    same = [meta[:, j : j + 1] for j in range(KC - 1)]

    @pl.loop(0, CONV // LANE)
    def _(k):
        x = proj[:, cols(k + DI // LANE)]
        tap = taps[:, cols(k)]
        dt = d_val[:, cols(k)] * d_act[:, cols(k)]
        g_taps[pl.ds(KC, 1), cols(k)] = jnp.sum(dt, axis=0, keepdims=True)
        g_taps[pl.ds(KC - 1, 1), cols(k)] = jnp.sum(dt * x, axis=0, keepdims=True)
        dc = dt * tap[KC - 1 : KC]
        for j in range(1, KC):
            ds_j = dt * same[j - 1]
            g_taps[pl.ds(KC - 1 - j, 1), cols(k)] = jnp.sum(
                ds_j * pltpu.roll(x, j, 0), axis=0, keepdims=True
            )
            dc = dc + pltpu.roll(ds_j, n - j, 0) * tap[KC - 1 - j : KC - j]
        d_proj_b[:, cols(k + DI // LANE)] = dc.astype(BF16)

    wide = 3 * LANE

    def add(k, total):
        return total + dot(d_proj_b[:, cols(k, wide)], w_in[:, cols(k, wide)], ((1,), (1,)))

    d_normed = lax.fori_loop(0, d_proj_b.shape[1] // wide, add, jnp.zeros((n, d), F32))
    g_gain[...] = jnp.sum(d_normed * h * root, axis=0, keepdims=True)
    u = d_normed * gain[...]
    back = jnp.sum(u * h, axis=-1, keepdims=True) * (root * root * root) / d
    grad_hidden[...] = upstream[...] + root * u - h * back


def per_device(
    hidden_in, cotangent, seq_ids, norm_gain, in_weight, conv_weight, conv_bias, out_gain,
    out_weight, decay_log, skip_gain, step_bias,
):
    n, d = hidden_in.shape
    rows, width = in_weight.shape
    padded = -(-width // LANE) * LANE
    spare = padded - width
    small = jnp.concatenate([norm_gain, conv_weight.reshape(-1), conv_bias, out_gain])
    packed = jnp.pad(small, (0, rows * spare - small.shape[0])).reshape(rows, spare)
    sent = jnp.concatenate([in_weight, packed], axis=1)
    w_in = lax.all_gather(sent, AXES, axis=0, tiled=True)
    w_out = lax.all_gather(out_weight, AXES, axis=0, tiled=True)
    devices = w_in.shape[0] // rows
    table = w_in[:, width:].reshape(devices, rows * spare).astype(F32)
    sizes = [norm_gain.shape[0]] + [conv_bias.shape[0]] * (KC + 1) + [out_gain.shape[0]]
    parts, at = [], 0
    for size in sizes:
        parts.append(table[:, at : at + size].reshape(1, -1))
        at += size
    gain = parts[0]
    taps = jnp.concatenate(parts[1 : KC + 2] + [jnp.zeros((8 - KC - 1, CONV), F32)])
    o_gain = parts[KC + 2]
    skip_e = jnp.repeat(skip_gain, HD)[None]
    heads = jnp.pad(jnp.stack([step_bias, -jnp.exp(decay_log)]), ((0, 6), (0, LANE - NH)))
    matched = [
        jnp.concatenate([jnp.zeros((j,), F32), (seq_ids[j:] == seq_ids[:-j]).astype(F32)])
        for j in range(1, KC)
    ]
    meta = jnp.stack(matched + [(seq_ids >= 0).astype(F32)], axis=1)
    seq_col, seq_row = seq_ids[:, None], seq_ids[None]
    limit = pltpu.CompilerParams(vmem_limit_bytes=56 * 1024 * 1024)

    saved = pl.pallas_call(
        forward_kernel,
        name="forward",
        out_shape=[
            sds(n, d, dtype=BF16), sds(n, padded), sds(n, CONV), sds(n, CONV), sds(n, DI),
            sds(n, DI, dtype=BF16), sds(n, DI), sds(n, LANE), sds(n, LANE), sds(n, DI),
            sds(n, DI), sds(LANE, n), sds(n, n),
        ],
        in_specs=[VM] * 10,
        out_specs=[VM] * 13,
        compiler_params=limit,
        cost_estimate=pl.CostEstimate(flops=4 * 10**9, bytes_accessed=10**7, transcendentals=10**6),
    )(hidden_in, w_in, gain, taps, o_gain, skip_e, heads, meta, seq_col, seq_row)
    normed_b, proj, act, d_act, inner, mixed_b, gated, stats, step, step_e, cum_e, cum_t, scores = saved
    rows_first = (((0,), (0,)), ((), ()))
    grad_out = lax.dot_general(
        mixed_b, cotangent.astype(BF16), rows_first, preferred_element_type=F32
    ).astype(BF16)
    own_out = lax.psum_scatter(grad_out, AXES, scatter_dimension=0, tiled=True)

    grad_hidden, d_proj_b, g_gain, g_taps, g_out, g_heads = pl.pallas_call(
        backward_kernel,
        name="backward",
        out_shape=[
            sds(n, d), sds(n, padded, dtype=BF16), sds(1, d), sds(8, CONV), sds(1, DI), sds(8, LANE),
        ],
        in_specs=[VM] * 23,
        out_specs=[VM] * 6,
        scratch_shapes=[
            pltpu.VMEM((n, CONV), F32), pltpu.VMEM((n, DI), F32), pltpu.VMEM((n, LANE), F32),
            pltpu.VMEM((n, n), F32),
        ],
        compiler_params=limit,
        cost_estimate=pl.CostEstimate(flops=8 * 10**9, bytes_accessed=10**7, transcendentals=10**6),
    )(
        hidden_in, cotangent, w_in, w_out, gain, taps, o_gain, skip_e, heads, meta, seq_col, seq_row,
        proj, act, d_act, inner, gated, stats, step, step_e, cum_e, cum_t, scores,
    )
    pieces = [g_gain] + [g_taps[j : j + 1] for j in range(KC + 1)] + [g_out]
    table = jnp.concatenate([p.reshape(devices, -1) for p in pieces], axis=1)
    table = jnp.pad(table, ((0, 0), (0, rows * spare - table.shape[1])))
    table = jnp.pad(table.reshape(devices * rows, spare), ((0, 0), (width, 0)))
    grad_in = lax.dot_general(normed_b, d_proj_b, rows_first, preferred_element_type=F32)
    own = lax.psum_scatter(
        (grad_in + table).astype(BF16), AXES, scatter_dimension=0, tiled=True
    ).astype(F32)
    block_out = hidden_in + jnp.dot(mixed_b, w_out, preferred_element_type=F32)
    head_sums = lax.psum(g_heads, AXES)
    tail = own[:, width:].reshape(-1)
    outs, at = [], 0
    for size in sizes:
        outs.append(tail[at : at + size])
        at += size
    return (
        block_out,
        grad_hidden,
        outs[0],
        own[:, :width],
        jnp.stack(outs[1 : KC + 1]),
        outs[KC + 1],
        outs[KC + 2],
        own_out.astype(F32),
        head_sums[0, :NH],
        head_sums[1, :NH],
        head_sums[2, :NH],
    )


def solution(mesh):
    rows, flat = P(AXES, None), P(AXES)
    return jax.shard_map(
        per_device,
        mesh=mesh,
        in_specs=(rows, rows, flat, flat, rows, P(None, AXES), flat, flat, rows, P(), P(), P()),
        out_specs=(rows, rows, flat, rows, P(None, AXES), flat, flat, rows, P(), P(), P()),
        check_vma=False,
    )
```

```python
import jax
import jax.numpy as jnp
from jax import lax
from jax.experimental import pallas as pl
from jax.experimental.pallas import tpu as pltpu
from jax.sharding import PartitionSpec as P

NS = 128
HD = 64
NH = 24
KC = 4
DI = 1536
CONV = 1792
LANE = 128
EPS = 1e-05
AXES = ("dp", "fsdp")
F32 = jnp.float32
BF16 = jnp.bfloat16
HIGH = lax.Precision.HIGHEST
VM = pl.BlockSpec(memory_space=pltpu.VMEM)


def sds(*shape, dtype=F32):
    return jax.ShapeDtypeStruct(shape, dtype)


def cols(k, width=LANE):
    return pl.ds(pl.multiple_of(k * width, LANE), width)


def sigmoid(x):
    return 1.0 / (1.0 + jnp.exp(-x))


def dot(a, b, dims=((1,), (0,)), precision=None):
    return lax.dot_general(
        a, b, (dims, ((), ())), precision=precision, preferred_element_type=F32
    )


def pair_masks():
    lane = lax.broadcasted_iota(jnp.int32, (1, LANE), 1)
    first = (lane < HD).astype(F32)
    return first, 1.0 - first


def spread(width_from, k):
    head = lax.broadcasted_iota(jnp.int32, (width_from, LANE), 0)
    lane = lax.broadcasted_iota(jnp.int32, (width_from, LANE), 1)
    return (head == 2 * k + lane // HD).astype(F32)


def pair_decay(cum_e, cum_t, k, mask):
    two = cum_e[:, cols(k)]
    low = jnp.float32(-1e30)
    first = two[:, 0:1] - cum_t[pl.ds(2 * k, 1), :]
    second = two[:, HD : HD + 1] - cum_t[pl.ds(2 * k + 1, 1), :]
    return jnp.exp(jnp.where(mask, first, low)), jnp.exp(jnp.where(mask, second, low))


def same_mask(seq_col, seq_row):
    n = seq_col.shape[0]
    row = lax.broadcasted_iota(jnp.int32, (n, n), 0)
    col = lax.broadcasted_iota(jnp.int32, (n, n), 1)
    return (seq_col[...] == seq_row[...]) & (row >= col)


def forward_kernel(
    hidden, w_in, gain, taps, out_gain, skip_e, heads, meta, seq_col, seq_row,
    normed_b, proj, act, d_act, inner, mixed_b, gated, stats, step, step_e, cum_e, cum_t, scores,
):
    h = hidden[...]
    n, d = h.shape
    root = lax.rsqrt(jnp.sum(h * h, axis=-1, keepdims=True) / d + EPS)
    nb = (h * root * gain[...]).astype(BF16)
    normed_b[...] = nb
    wide = 3 * LANE

    @pl.loop(0, proj.shape[1] // wide)
    def _(k):
        proj[:, cols(k, wide)] = dot(nb, w_in[:, cols(k, wide)])

    same = [meta[:, j : j + 1] for j in range(KC - 1)]

    @pl.loop(0, CONV // LANE)
    def _(k):
        x = proj[:, cols(k + DI // LANE)]
        tap = taps[:, cols(k)]
        total = tap[KC : KC + 1] + x * tap[KC - 1 : KC]
        for j in range(1, KC):
            total = total + pltpu.roll(x, j, 0) * same[j - 1] * tap[KC - 1 - j : KC - j]
        sg = sigmoid(total)
        act[:, cols(k)] = total * sg
        d_act[:, cols(k)] = sg * (1.0 + total * (1.0 - sg))

    mask = same_mask(seq_col, seq_row)
    raw = proj[:, DI + CONV : DI + CONV + LANE] + heads[0:1]
    lane = lax.broadcasted_iota(jnp.int32, (1, LANE), 1)
    size = jnp.where(
        lane < NH, jnp.maximum(raw, 0.0) + jnp.log1p(jnp.exp(-jnp.abs(raw))), 0.0
    )
    step[...] = size
    running = dot(mask.astype(F32), size * heads[1:2], precision=HIGH)
    cum_t[...] = running.T
    b = act[:, DI : DI + NS].astype(BF16)
    c = act[:, DI + NS : DI + 2 * NS].astype(BF16)
    scores[...] = dot(c, b, ((1,), (1,)))
    first, second = pair_masks()
    stats[...] = jnp.zeros_like(stats)

    @pl.loop(0, NH // 2)
    def _(k):
        e = spread(LANE, k)
        cum_e[:, cols(k)] = dot(running, e, precision=HIGH)
        size_e = dot(size, e, precision=HIGH)
        step_e[:, cols(k)] = size_e
        decay0, decay1 = pair_decay(cum_e, cum_t, k, mask)
        v = act[:, cols(k)]
        x = v * size_e
        s = scores[...]
        y = dot((s * decay0).astype(BF16), (x * first).astype(BF16)) + dot(
            (s * decay1).astype(BF16), (x * second).astype(BF16)
        )
        inner[:, cols(k)] = y
        g = proj[:, cols(k)]
        z = (y + skip_e[:, cols(k)] * v) * g * sigmoid(g)
        gated[:, cols(k)] = z
        stats[...] += z * z

    scale = lax.rsqrt(jnp.sum(stats[...], axis=-1, keepdims=True) / DI + EPS)
    live = meta[:, KC - 1 : KC]
    stats[...] = jnp.where(lane < HD, scale, root)
    factor = scale * live

    @pl.loop(0, NH // 2)
    def _(k):
        mixed_b[:, cols(k)] = (gated[:, cols(k)] * factor * out_gain[:, cols(k)]).astype(BF16)


def backward_kernel(
    hidden, upstream, w_in, w_out, gain, taps, out_gain, skip_e, heads, meta, seq_col, seq_row,
    proj, act, d_act, inner, gated, stats, step, step_e, cum_e, cum_t, scores,
    grad_hidden, d_proj_b, g_gain, g_taps, g_out, g_heads,
    d_val, d_gated, acc, d_scores,
):
    h = hidden[...]
    n, d = h.shape
    up = upstream[...].astype(BF16)
    mask = same_mask(seq_col, seq_row)
    live = meta[:, KC - 1 : KC]
    scale = stats[:, 0:1]
    root = stats[:, HD : HD + 1]
    first, second = pair_masks()
    acc[...] = jnp.zeros_like(acc)

    @pl.loop(0, NH // 2)
    def _(k):
        dm = dot(up, w_out[cols(k), :], ((1,), (1,))) * live
        z = gated[:, cols(k)]
        g_out[:, cols(k)] = jnp.sum(dm * z * scale, axis=0, keepdims=True)
        u = dm * out_gain[:, cols(k)]
        d_gated[:, cols(k)] = u
        acc[...] += u * z

    pull = jnp.sum(acc[...], axis=-1, keepdims=True) * (scale * scale * scale) / DI
    d_scores[...] = jnp.zeros_like(d_scores)
    g_heads[...] = jnp.zeros_like(g_heads)
    tall = lax.broadcasted_iota(jnp.int32, (8, 1), 0)

    def body(k, carry):
        d_cum, d_step = carry
        e = spread(LANE, k)
        dz = scale * d_gated[:, cols(k)] - gated[:, cols(k)] * pull
        g = proj[:, cols(k)]
        sg = sigmoid(g)
        v = act[:, cols(k)]
        y = inner[:, cols(k)]
        skip = skip_e[:, cols(k)]
        d_proj_b[:, cols(k)] = (
            dz * (y + skip * v) * sg * (1.0 + g * (1.0 - sg))
        ).astype(BF16)
        dy = dz * g * sg
        size_e = step_e[:, cols(k)]
        x = (v * size_e).astype(BF16)
        dyb = dy.astype(BF16)
        dy0 = (dy * first).astype(BF16)
        dy1 = (dy * second).astype(BF16)
        decay0, decay1 = pair_decay(cum_e, cum_t, k, mask)
        s = scores[...]
        dx = dot((s * decay0).astype(BF16), dy0, ((0,), (0,))) + dot(
            (s * decay1).astype(BF16), dy1, ((0,), (0,))
        )
        d_scores[...] += dot(dy0, x, ((1,), (1,))) * decay0 + dot(dy1, x, ((1,), (1,))) * decay1
        d_val[:, cols(k)] = dx * size_e + skip * dy
        flow = dyb.astype(F32) * y - x.astype(F32) * dx
        d_cum = d_cum + dot(flow, e, ((1,), (1,)), precision=HIGH)
        d_step = d_step + dot(dx * v, e, ((1,), (1,)), precision=HIGH)
        skips = jnp.sum(dy * v, axis=0, keepdims=True)
        g_heads[...] += jnp.where(
            tall == 1, dot(jnp.broadcast_to(skips, (8, LANE)), e, ((1,), (1,)), precision=HIGH), 0.0
        )
        return d_cum, d_step

    zero = jnp.zeros((n, LANE), F32)
    d_cum, d_step = lax.fori_loop(0, NH // 2, body, (zero, zero))
    d_rate = dot(mask.astype(F32), d_cum, ((0,), (0,)), precision=HIGH)
    neg = heads[1:2]
    size = step[...]
    raw = proj[:, DI + CONV : DI + CONV + LANE] + heads[0:1]
    lane = lax.broadcasted_iota(jnp.int32, (1, LANE), 1)
    d_raw = jnp.where(lane < NH, (d_step + d_rate * neg) * sigmoid(raw), 0.0)
    d_proj_b[:, DI + CONV : DI + CONV + LANE] = d_raw.astype(BF16)
    g_decay = jnp.sum(d_rate * size * neg, axis=0, keepdims=True)
    g_step = jnp.sum(d_raw, axis=0, keepdims=True)
    g_heads[...] += jnp.where(tall == 0, g_decay, 0.0) + jnp.where(tall == 2, g_step, 0.0)

    b = act[:, DI : DI + NS].astype(BF16)
    c = act[:, DI + NS : DI + 2 * NS].astype(BF16)
    ds = d_scores[...].astype(BF16)
    d_val[:, DI : DI + NS] = dot(ds, c, ((0,), (0,)))
    d_val[:, DI + NS : DI + 2 * NS] = dot(ds, b)
    same = [meta[:, j : j + 1] for j in range(KC - 1)]

    @pl.loop(0, CONV // LANE)
    def _(k):
        x = proj[:, cols(k + DI // LANE)]
        tap = taps[:, cols(k)]
        dt = d_val[:, cols(k)] * d_act[:, cols(k)]
        g_taps[pl.ds(KC, 1), cols(k)] = jnp.sum(dt, axis=0, keepdims=True)
        g_taps[pl.ds(KC - 1, 1), cols(k)] = jnp.sum(dt * x, axis=0, keepdims=True)
        dc = dt * tap[KC - 1 : KC]
        for j in range(1, KC):
            ds_j = dt * same[j - 1]
            g_taps[pl.ds(KC - 1 - j, 1), cols(k)] = jnp.sum(
                ds_j * pltpu.roll(x, j, 0), axis=0, keepdims=True
            )
            dc = dc + pltpu.roll(ds_j, n - j, 0) * tap[KC - 1 - j : KC - j]
        d_proj_b[:, cols(k + DI // LANE)] = dc.astype(BF16)

    wide = 3 * LANE

    def add(k, total):
        return total + dot(d_proj_b[:, cols(k, wide)], w_in[:, cols(k, wide)], ((1,), (1,)))

    d_normed = lax.fori_loop(0, d_proj_b.shape[1] // wide, add, jnp.zeros((n, d), F32))
    g_gain[...] = jnp.sum(d_normed * h * root, axis=0, keepdims=True)
    u = d_normed * gain[...]
    back = jnp.sum(u * h, axis=-1, keepdims=True) * (root * root * root) / d
    grad_hidden[...] = upstream[...] + root * u - h * back


def per_device(
    hidden_in, cotangent, seq_ids, norm_gain, in_weight, conv_weight, conv_bias, out_gain,
    out_weight, decay_log, skip_gain, step_bias,
):
    n, d = hidden_in.shape
    rows, width = in_weight.shape
    padded = -(-width // LANE) * LANE
    spare = padded - width
    small = jnp.concatenate([norm_gain, conv_weight.reshape(-1), conv_bias, out_gain])
    packed = jnp.pad(small, (0, rows * spare - small.shape[0])).reshape(rows, spare)
    folds = out_weight.shape[0] // rows
    halves = [out_weight[j * rows : (j + 1) * rows] for j in range(folds)]
    sent = jnp.concatenate([in_weight, packed] + halves, axis=1)
    w_in = lax.all_gather(sent, AXES, axis=0, tiled=True)
    devices = w_in.shape[0] // rows
    w_out = jnp.stack(
        [w_in[:, padded + j * d : padded + (j + 1) * d].reshape(devices, rows, d) for j in range(folds)],
        axis=1,
    ).reshape(-1, d)
    table = w_in[:, width:padded].reshape(devices, rows * spare).astype(F32)
    sizes = [norm_gain.shape[0]] + [conv_bias.shape[0]] * (KC + 1) + [out_gain.shape[0]]
    parts, at = [], 0
    for size in sizes:
        parts.append(table[:, at : at + size].reshape(1, -1))
        at += size
    gain = parts[0]
    taps = jnp.concatenate(parts[1 : KC + 2] + [jnp.zeros((8 - KC - 1, CONV), F32)])
    o_gain = parts[KC + 2]
    skip_e = jnp.repeat(skip_gain, HD)[None]
    heads = jnp.pad(jnp.stack([step_bias, -jnp.exp(decay_log)]), ((0, 6), (0, LANE - NH)))
    matched = [
        jnp.concatenate([jnp.zeros((j,), F32), (seq_ids[j:] == seq_ids[:-j]).astype(F32)])
        for j in range(1, KC)
    ]
    meta = jnp.stack(matched + [(seq_ids >= 0).astype(F32)], axis=1)
    seq_col, seq_row = seq_ids[:, None], seq_ids[None]
    limit = pltpu.CompilerParams(vmem_limit_bytes=56 * 1024 * 1024)

    saved = pl.pallas_call(
        forward_kernel,
        name="forward",
        out_shape=[
            sds(n, d, dtype=BF16), sds(n, padded), sds(n, CONV), sds(n, CONV), sds(n, DI),
            sds(n, DI, dtype=BF16), sds(n, DI), sds(n, LANE), sds(n, LANE), sds(n, DI),
            sds(n, DI), sds(LANE, n), sds(n, n),
        ],
        in_specs=[VM] * 10,
        out_specs=[VM] * 13,
        compiler_params=limit,
        cost_estimate=pl.CostEstimate(flops=4 * 10**9, bytes_accessed=10**7, transcendentals=10**6),
    )(hidden_in, w_in, gain, taps, o_gain, skip_e, heads, meta, seq_col, seq_row)
    normed_b, proj, act, d_act, inner, mixed_b, gated, stats, step, step_e, cum_e, cum_t, scores = saved
    rows_first = (((0,), (0,)), ((), ()))
    grad_out = lax.dot_general(
        mixed_b, cotangent.astype(BF16), rows_first, preferred_element_type=F32
    ).astype(BF16)

    grad_hidden, d_proj_b, g_gain, g_taps, g_out, g_heads = pl.pallas_call(
        backward_kernel,
        name="backward",
        out_shape=[
            sds(n, d), sds(n, padded, dtype=BF16), sds(1, d), sds(8, CONV), sds(1, DI), sds(8, LANE),
        ],
        in_specs=[VM] * 23,
        out_specs=[VM] * 6,
        scratch_shapes=[
            pltpu.VMEM((n, CONV), F32), pltpu.VMEM((n, DI), F32), pltpu.VMEM((n, LANE), F32),
            pltpu.VMEM((n, n), F32),
        ],
        compiler_params=limit,
        cost_estimate=pl.CostEstimate(flops=8 * 10**9, bytes_accessed=10**7, transcendentals=10**6),
    )(
        hidden_in, cotangent, w_in, w_out, gain, taps, o_gain, skip_e, heads, meta, seq_col, seq_row,
        proj, act, d_act, inner, gated, stats, step, step_e, cum_e, cum_t, scores,
    )
    pieces = [g_gain] + [g_taps[j : j + 1] for j in range(KC + 1)] + [g_out]
    table = jnp.concatenate([p.reshape(devices, -1) for p in pieces], axis=1)
    table = jnp.pad(table, ((0, 0), (0, rows * spare - table.shape[1])))
    table = jnp.pad(table.reshape(devices * rows, spare), ((0, 0), (width, 0)))
    grad_in = lax.dot_general(normed_b, d_proj_b, rows_first, preferred_element_type=F32)
    split = grad_out.reshape(devices, folds, rows, d)
    partial = jnp.concatenate(
        [(grad_in + table).astype(BF16)] + [split[:, j].reshape(-1, d) for j in range(folds)], axis=1
    )
    partial, g_heads = lax.optimization_barrier((partial, g_heads))
    own = lax.psum_scatter(partial, AXES, scatter_dimension=0, tiled=True).astype(F32)
    own_out = jnp.concatenate(
        [own[:, padded + j * d : padded + (j + 1) * d] for j in range(folds)], axis=0
    )
    block_out = hidden_in + jnp.dot(mixed_b, w_out, preferred_element_type=F32)
    head_sums = lax.psum(g_heads, AXES)
    tail = own[:, width:padded].reshape(-1)
    outs, at = [], 0
    for size in sizes:
        outs.append(tail[at : at + size])
        at += size
    return (
        block_out,
        grad_hidden,
        outs[0],
        own[:, :width],
        jnp.stack(outs[1 : KC + 1]),
        outs[KC + 1],
        outs[KC + 2],
        own_out,
        head_sums[0, :NH],
        head_sums[1, :NH],
        head_sums[2, :NH],
    )


def solution(mesh):
    rows, flat = P(AXES, None), P(AXES)
    return jax.shard_map(
        per_device,
        mesh=mesh,
        in_specs=(rows, rows, flat, flat, rows, P(None, AXES), flat, flat, rows, P(), P(), P()),
        out_specs=(rows, rows, flat, rows, P(None, AXES), flat, flat, rows, P(), P(), P()),
        check_vma=False,
    )
```

```python
import jax
import jax.numpy as jnp
from jax import lax
from jax.experimental import pallas as pl
from jax.experimental.pallas import tpu as pltpu
from jax.sharding import PartitionSpec as P

NS = 128
HD = 64
NH = 24
KC = 4
DI = 1536
CONV = 1792
LANE = 128
EPS = 1e-05
AXES = ("dp", "fsdp")
F32 = jnp.float32
BF16 = jnp.bfloat16
HIGH = lax.Precision.HIGHEST
VM = pl.BlockSpec(memory_space=pltpu.VMEM)


def sds(*shape, dtype=F32):
    return jax.ShapeDtypeStruct(shape, dtype)


def cols(k, width=LANE):
    return pl.ds(pl.multiple_of(k * width, LANE), width)


def sigmoid(x):
    return 1.0 / (1.0 + jnp.exp(-x))


def dot(a, b, dims=((1,), (0,)), precision=None):
    return lax.dot_general(
        a, b, (dims, ((), ())), precision=precision, preferred_element_type=F32
    )


def pair_masks():
    lane = lax.broadcasted_iota(jnp.int32, (1, LANE), 1)
    first = (lane < HD).astype(F32)
    return first, 1.0 - first


def spread(width_from, k):
    head = lax.broadcasted_iota(jnp.int32, (width_from, LANE), 0)
    lane = lax.broadcasted_iota(jnp.int32, (width_from, LANE), 1)
    return (head == 2 * k + lane // HD).astype(F32)


def pair_decay(cum_e, cum_t, k, mask):
    two = cum_e[:, cols(k)]
    low = jnp.float32(-1e30)
    first = two[:, 0:1] - cum_t[pl.ds(2 * k, 1), :]
    second = two[:, HD : HD + 1] - cum_t[pl.ds(2 * k + 1, 1), :]
    return jnp.exp(jnp.where(mask, first, low)), jnp.exp(jnp.where(mask, second, low))


def same_mask(seq_col, seq_row):
    n = seq_col.shape[0]
    row = lax.broadcasted_iota(jnp.int32, (n, n), 0)
    col = lax.broadcasted_iota(jnp.int32, (n, n), 1)
    return (seq_col[...] == seq_row[...]) & (row >= col)


def forward_kernel(
    hidden, w_in, gain, taps, out_gain, skip_e, heads, meta, seq_col, seq_row,
    normed_b, proj, act, d_act, inner, mixed_b, gated, stats, step, step_e, cum_e, cum_t, scores,
):
    h = hidden[...]
    n, d = h.shape
    root = lax.rsqrt(jnp.sum(h * h, axis=-1, keepdims=True) / d + EPS)
    nb = (h * root * gain[...]).astype(BF16)
    normed_b[...] = nb
    wide = 3 * LANE

    @pl.loop(0, proj.shape[1] // wide)
    def _(k):
        proj[:, cols(k, wide)] = dot(nb, w_in[:, cols(k, wide)])

    same = [meta[:, j : j + 1] for j in range(KC - 1)]

    @pl.loop(0, CONV // LANE)
    def _(k):
        x = proj[:, cols(k + DI // LANE)]
        tap = taps[:, cols(k)]
        total = tap[KC : KC + 1] + x * tap[KC - 1 : KC]
        for j in range(1, KC):
            total = total + pltpu.roll(x, j, 0) * same[j - 1] * tap[KC - 1 - j : KC - j]
        sg = sigmoid(total)
        act[:, cols(k)] = total * sg
        d_act[:, cols(k)] = sg * (1.0 + total * (1.0 - sg))

    mask = same_mask(seq_col, seq_row)
    raw = proj[:, DI + CONV : DI + CONV + LANE] + heads[0:1]
    lane = lax.broadcasted_iota(jnp.int32, (1, LANE), 1)
    size = jnp.where(
        lane < NH, jnp.maximum(raw, 0.0) + jnp.log1p(jnp.exp(-jnp.abs(raw))), 0.0
    )
    step[...] = size
    running = dot(mask.astype(F32), size * heads[1:2], precision=HIGH)
    cum_t[...] = running.T
    b = act[:, DI : DI + NS].astype(BF16)
    c = act[:, DI + NS : DI + 2 * NS].astype(BF16)
    scores[...] = dot(c, b, ((1,), (1,)))
    first, second = pair_masks()
    stats[...] = jnp.zeros_like(stats)

    @pl.loop(0, NH // 2)
    def _(k):
        e = spread(LANE, k)
        cum_e[:, cols(k)] = dot(running, e, precision=HIGH)
        size_e = dot(size, e, precision=HIGH)
        step_e[:, cols(k)] = size_e
        decay0, decay1 = pair_decay(cum_e, cum_t, k, mask)
        v = act[:, cols(k)]
        x = v * size_e
        s = scores[...]
        y = dot((s * decay0).astype(BF16), (x * first).astype(BF16)) + dot(
            (s * decay1).astype(BF16), (x * second).astype(BF16)
        )
        inner[:, cols(k)] = y
        g = proj[:, cols(k)]
        z = (y + skip_e[:, cols(k)] * v) * g * sigmoid(g)
        gated[:, cols(k)] = z
        stats[...] += z * z

    scale = lax.rsqrt(jnp.sum(stats[...], axis=-1, keepdims=True) / DI + EPS)
    live = meta[:, KC - 1 : KC]
    stats[...] = jnp.where(lane < HD, scale, root)
    factor = scale * live

    @pl.loop(0, NH // 2)
    def _(k):
        mixed_b[:, cols(k)] = (gated[:, cols(k)] * factor * out_gain[:, cols(k)]).astype(BF16)


def backward_kernel(
    hidden, upstream, w_in, w_out, gain, taps, out_gain, skip_e, heads, meta, seq_col, seq_row,
    proj, act, d_act, inner, gated, stats, step, step_e, cum_e, cum_t, scores,
    grad_hidden, d_proj_b, g_gain, g_taps, g_out, g_heads,
    d_val, d_gated, acc, d_scores,
):
    h = hidden[...]
    n, d = h.shape
    up = upstream[...].astype(BF16)
    mask = same_mask(seq_col, seq_row)
    live = meta[:, KC - 1 : KC]
    scale = stats[:, 0:1]
    root = stats[:, HD : HD + 1]
    first, second = pair_masks()
    acc[...] = jnp.zeros_like(acc)

    @pl.loop(0, NH // 2)
    def _(k):
        dm = dot(up, w_out[cols(k), :], ((1,), (1,))) * live
        z = gated[:, cols(k)]
        g_out[:, cols(k)] = jnp.sum(dm * z * scale, axis=0, keepdims=True)
        u = dm * out_gain[:, cols(k)]
        d_gated[:, cols(k)] = u
        acc[...] += u * z

    pull = jnp.sum(acc[...], axis=-1, keepdims=True) * (scale * scale * scale) / DI
    d_scores[...] = jnp.zeros_like(d_scores)
    g_heads[...] = jnp.zeros_like(g_heads)
    tall = lax.broadcasted_iota(jnp.int32, (8, 1), 0)

    def body(k, carry):
        d_cum, d_step = carry
        e = spread(LANE, k)
        dz = scale * d_gated[:, cols(k)] - gated[:, cols(k)] * pull
        g = proj[:, cols(k)]
        sg = sigmoid(g)
        v = act[:, cols(k)]
        y = inner[:, cols(k)]
        skip = skip_e[:, cols(k)]
        d_proj_b[:, cols(k)] = (
            dz * (y + skip * v) * sg * (1.0 + g * (1.0 - sg))
        ).astype(BF16)
        dy = dz * g * sg
        size_e = step_e[:, cols(k)]
        x = (v * size_e).astype(BF16)
        dyb = dy.astype(BF16)
        dy0 = (dy * first).astype(BF16)
        dy1 = (dy * second).astype(BF16)
        decay0, decay1 = pair_decay(cum_e, cum_t, k, mask)
        s = scores[...]
        dx = dot((s * decay0).astype(BF16), dy0, ((0,), (0,))) + dot(
            (s * decay1).astype(BF16), dy1, ((0,), (0,))
        )
        d_scores[...] += dot(dy0, x, ((1,), (1,))) * decay0 + dot(dy1, x, ((1,), (1,))) * decay1
        d_val[:, cols(k)] = dx * size_e + skip * dy
        flow = dyb.astype(F32) * y - x.astype(F32) * dx
        d_cum = d_cum + dot(flow, e, ((1,), (1,)), precision=HIGH)
        d_step = d_step + dot(dx * v, e, ((1,), (1,)), precision=HIGH)
        skips = jnp.sum(dy * v, axis=0, keepdims=True)
        g_heads[...] += jnp.where(
            tall == 1, dot(jnp.broadcast_to(skips, (8, LANE)), e, ((1,), (1,)), precision=HIGH), 0.0
        )
        return d_cum, d_step

    zero = jnp.zeros((n, LANE), F32)
    d_cum, d_step = lax.fori_loop(0, NH // 2, body, (zero, zero))
    d_rate = dot(mask.astype(F32), d_cum, ((0,), (0,)), precision=HIGH)
    neg = heads[1:2]
    size = step[...]
    raw = proj[:, DI + CONV : DI + CONV + LANE] + heads[0:1]
    lane = lax.broadcasted_iota(jnp.int32, (1, LANE), 1)
    d_raw = jnp.where(lane < NH, (d_step + d_rate * neg) * sigmoid(raw), 0.0)
    d_proj_b[:, DI + CONV : DI + CONV + LANE] = d_raw.astype(BF16)
    g_decay = jnp.sum(d_rate * size * neg, axis=0, keepdims=True)
    g_step = jnp.sum(d_raw, axis=0, keepdims=True)
    g_heads[...] += jnp.where(tall == 0, g_decay, 0.0) + jnp.where(tall == 2, g_step, 0.0)

    b = act[:, DI : DI + NS].astype(BF16)
    c = act[:, DI + NS : DI + 2 * NS].astype(BF16)
    ds = d_scores[...].astype(BF16)
    d_val[:, DI : DI + NS] = dot(ds, c, ((0,), (0,)))
    d_val[:, DI + NS : DI + 2 * NS] = dot(ds, b)
    same = [meta[:, j : j + 1] for j in range(KC - 1)]

    @pl.loop(0, CONV // LANE)
    def _(k):
        x = proj[:, cols(k + DI // LANE)]
        tap = taps[:, cols(k)]
        dt = d_val[:, cols(k)] * d_act[:, cols(k)]
        g_taps[pl.ds(KC, 1), cols(k)] = jnp.sum(dt, axis=0, keepdims=True)
        g_taps[pl.ds(KC - 1, 1), cols(k)] = jnp.sum(dt * x, axis=0, keepdims=True)
        dc = dt * tap[KC - 1 : KC]
        for j in range(1, KC):
            ds_j = dt * same[j - 1]
            g_taps[pl.ds(KC - 1 - j, 1), cols(k)] = jnp.sum(
                ds_j * pltpu.roll(x, j, 0), axis=0, keepdims=True
            )
            dc = dc + pltpu.roll(ds_j, n - j, 0) * tap[KC - 1 - j : KC - j]
        d_proj_b[:, cols(k + DI // LANE)] = dc.astype(BF16)

    wide = 3 * LANE

    def add(k, total):
        return total + dot(d_proj_b[:, cols(k, wide)], w_in[:, cols(k, wide)], ((1,), (1,)))

    d_normed = lax.fori_loop(0, d_proj_b.shape[1] // wide, add, jnp.zeros((n, d), F32))
    g_gain[...] = jnp.sum(d_normed * h * root, axis=0, keepdims=True)
    u = d_normed * gain[...]
    back = jnp.sum(u * h, axis=-1, keepdims=True) * (root * root * root) / d
    grad_hidden[...] = upstream[...] + root * u - h * back


def whole_kernel(
    hidden, upstream, w_in, w_out, gain, taps, out_gain, skip_e, heads, meta, seq_col, seq_row,
    normed_b, mixed_b, grad_hidden, d_proj_b, g_gain, g_taps, g_out, g_heads,
    proj, act, d_act, inner, gated, stats, step, step_e, cum_e, cum_t, scores,
    d_val, d_gated, acc, d_scores,
):
    shared = (gain, taps, out_gain, skip_e, heads, meta, seq_col, seq_row)
    forward_kernel(
        hidden, w_in, *shared,
        normed_b, proj, act, d_act, inner, mixed_b, gated, stats, step, step_e, cum_e, cum_t, scores,
    )
    backward_kernel(
        hidden, upstream, w_in, w_out, *shared,
        proj, act, d_act, inner, gated, stats, step, step_e, cum_e, cum_t, scores,
        grad_hidden, d_proj_b, g_gain, g_taps, g_out, g_heads,
        d_val, d_gated, acc, d_scores,
    )


def per_device(
    hidden_in, cotangent, seq_ids, norm_gain, in_weight, conv_weight, conv_bias, out_gain,
    out_weight, decay_log, skip_gain, step_bias,
):
    n, d = hidden_in.shape
    rows, width = in_weight.shape
    padded = -(-width // LANE) * LANE
    spare = padded - width
    small = jnp.concatenate([norm_gain, conv_weight.reshape(-1), conv_bias, out_gain])
    packed = jnp.pad(small, (0, rows * spare - small.shape[0])).reshape(rows, spare)
    folds = out_weight.shape[0] // rows
    halves = [out_weight[j * rows : (j + 1) * rows] for j in range(folds)]
    sent = jnp.concatenate([in_weight, packed] + halves, axis=1)
    w_in = lax.all_gather(sent, AXES, axis=0, tiled=True)
    devices = w_in.shape[0] // rows
    w_out = jnp.stack(
        [w_in[:, padded + j * d : padded + (j + 1) * d].reshape(devices, rows, d) for j in range(folds)],
        axis=1,
    ).reshape(-1, d)
    table = w_in[:, width:padded].reshape(devices, rows * spare).astype(F32)
    sizes = [norm_gain.shape[0]] + [conv_bias.shape[0]] * (KC + 1) + [out_gain.shape[0]]
    parts, at = [], 0
    for size in sizes:
        parts.append(table[:, at : at + size].reshape(1, -1))
        at += size
    gain = parts[0]
    taps = jnp.concatenate(parts[1 : KC + 2] + [jnp.zeros((8 - KC - 1, CONV), F32)])
    o_gain = parts[KC + 2]
    skip_e = jnp.repeat(skip_gain, HD)[None]
    heads = jnp.pad(jnp.stack([step_bias, -jnp.exp(decay_log)]), ((0, 6), (0, LANE - NH)))
    matched = [
        jnp.concatenate([jnp.zeros((j,), F32), (seq_ids[j:] == seq_ids[:-j]).astype(F32)])
        for j in range(1, KC)
    ]
    meta = jnp.stack(matched + [(seq_ids >= 0).astype(F32)], axis=1)
    seq_col, seq_row = seq_ids[:, None], seq_ids[None]
    limit = pltpu.CompilerParams(vmem_limit_bytes=56 * 1024 * 1024)

    rows_first = (((0,), (0,)), ((), ()))
    normed_b, mixed_b, grad_hidden, d_proj_b, g_gain, g_taps, g_out, g_heads = pl.pallas_call(
        whole_kernel,
        name="mixer",
        out_shape=[
            sds(n, d, dtype=BF16), sds(n, DI, dtype=BF16), sds(n, d), sds(n, padded, dtype=BF16),
            sds(1, d), sds(8, CONV), sds(1, DI), sds(8, LANE),
        ],
        in_specs=[VM] * 12,
        out_specs=[VM] * 8,
        scratch_shapes=[
            pltpu.VMEM(shape, F32)
            for shape in (
                (n, padded), (n, CONV), (n, CONV), (n, DI), (n, DI), (n, LANE), (n, LANE), (n, DI),
                (n, DI), (LANE, n), (n, n), (n, CONV), (n, DI), (n, LANE), (n, n),
            )
        ],
        compiler_params=limit,
        cost_estimate=pl.CostEstimate(
            flops=12 * 10**9, bytes_accessed=10**7, transcendentals=10**6
        ),
    )(
        hidden_in, cotangent, w_in, w_out, gain, taps, o_gain, skip_e, heads, meta, seq_col, seq_row
    )
    grad_out = lax.dot_general(
        mixed_b, cotangent.astype(BF16), rows_first, preferred_element_type=F32
    ).astype(BF16)
    pieces = [g_gain] + [g_taps[j : j + 1] for j in range(KC + 1)] + [g_out]
    table = jnp.concatenate([p.reshape(devices, -1) for p in pieces], axis=1)
    table = jnp.pad(table, ((0, 0), (0, rows * spare - table.shape[1])))
    table = jnp.pad(table.reshape(devices * rows, spare), ((0, 0), (width, 0)))
    grad_in = lax.dot_general(normed_b, d_proj_b, rows_first, preferred_element_type=F32)
    split = grad_out.reshape(devices, folds, rows, d)
    partial = jnp.concatenate(
        [(grad_in + table).astype(BF16)] + [split[:, j].reshape(-1, d) for j in range(folds)], axis=1
    )
    partial, g_heads = lax.optimization_barrier((partial, g_heads))
    own = lax.psum_scatter(partial, AXES, scatter_dimension=0, tiled=True).astype(F32)
    own_out = jnp.concatenate(
        [own[:, padded + j * d : padded + (j + 1) * d] for j in range(folds)], axis=0
    )
    block_out = hidden_in + jnp.dot(mixed_b, w_out, preferred_element_type=F32)
    head_sums = lax.psum(g_heads, AXES)
    tail = own[:, width:padded].reshape(-1)
    outs, at = [], 0
    for size in sizes:
        outs.append(tail[at : at + size])
        at += size
    return (
        block_out,
        grad_hidden,
        outs[0],
        own[:, :width],
        jnp.stack(outs[1 : KC + 1]),
        outs[KC + 1],
        outs[KC + 2],
        own_out,
        head_sums[0, :NH],
        head_sums[1, :NH],
        head_sums[2, :NH],
    )


def solution(mesh):
    rows, flat = P(AXES, None), P(AXES)
    return jax.shard_map(
        per_device,
        mesh=mesh,
        in_specs=(rows, rows, flat, flat, rows, P(None, AXES), flat, flat, rows, P(), P(), P()),
        out_specs=(rows, rows, flat, rows, P(None, AXES), flat, flat, rows, P(), P(), P()),
        check_vma=False,
    )
```
